256 devices in a mesh: cfg: 2 (over y_hi), seq: 128 (over y_lo, x, z, core).
Axes of the slice: x: 4, y: 4 (y_hi: 2, y_lo: 2; y = y_hi * 2 + y_lo), z: 8, core: 2. Of those that a mesh axis runs over, the one named last changes fastest.
Arguments:
- hidden: bfloat16 [2, 6144, 3072], P('cfg', 'seq'), may hold values from -3 to 3
- queries: bfloat16 [2, 6144, 2048], P('cfg', 'seq'), may hold values from -5 to 5
- key_proj: bfloat16 [2, 6144, 2048], P('cfg', 'seq'), may hold values from -5 to 5
- value_proj: bfloat16 [2, 6144, 2048], P('cfg', 'seq'), may hold values from -12 to 12
- norm_gain: float32 [2, 64], replicated, may hold values from 0.1 to 1.9
- norm_bias: float32 [2, 64], replicated, may hold values from -2 to 2
- positions: int32 [3, 6144], P(None, 'seq'), may hold values from 0 to 47
- text_len: int32 [2], P('cfg'), may hold values from 1 to 226
- time_embed: bfloat16 [512], replicated, may hold values from -6 to 6
- gate_table: bfloat16 [512, 3072], P(None, 'seq'), may hold values from -0.25 to 0.25
- mod_table: bfloat16 [512, 6144], P(None, 'seq'), may hold values from -0.25 to 0.25
- out_weight: bfloat16 [2048, 3072], P(None, ('cfg', 'seq')), may hold values from -0.125 to 0.125
- proj_weight: bfloat16 [3072, 64], replicated, may hold values from -0.109375 to 0.109375
- proj_bias: float32 [64], replicated, may hold values from -3 to 3
- latent: float32 [6144, 64], P('seq'), may hold values from -6 to 6
- solver_coef: float32 [2, 50], replicated, may hold values from 0.3 to 1.2
- step_index: int32 [1], replicated, may hold values from 0 to 49
Outputs:
- latent_next: float32 [6144, 64], P('seq', 'cfg')
The draws below stay inside these ranges and needn't reach their ends.
All inputs are finite; a program needn't handle non-finite values.
Results may differ from the reference program's by a relative error of at most 0.0072.
Values may be sent and summed in bfloat16 or wider, within the bound.
No kernel may reach another device: no remote copies, remote signals or barrier semaphores. Data moves between devices by JAX's collectives and lax.ppermute only.
A program may use at most 128 MiB of HBM per device.

```python
import math
import jax
import jax.numpy as jnp
import numpy as np
from jax import lax

D = 3072
HEADS = 32
HEAD_DIM = 64
TEMB = 512
CHANNELS = 64
TEXT = 226
TEXT_SLOTS = 256
STEPS = 50
TOKENS = 6144


noise_level = 0.15


def slow_mask():
    table = np.zeros((64,), np.float32)
    for pair_index in [4, 5, 6, 7, 14, 15, 16, 17, 18, 19, 26, 27, 28, 29, 30, 31]:
        table[2 * pair_index] = 1.0
        table[2 * pair_index + 1] = 1.0
    return jnp.asarray(table)


def cluster_shared(key):
    group_count = max(TOKENS // 8, 1)
    cluster_ids = jax.random.randint(jax.random.fold_in(key, 11), (2, TOKENS, HEADS), 0, group_count)
    centres = jax.random.normal(jax.random.fold_in(key, 12), (2, group_count, HEADS, HEAD_DIM), jnp.float32)
    centres = jnp.clip(centres, -4.0, 4.0)
    half_index = jnp.arange(2)[:, None, None]
    head_index = jnp.arange(HEADS)[None, None, :]
    shared_part = centres[half_index, cluster_ids, head_index]
    return shared_part * slow_mask()[None, None, None, :]


def draw_queries(key, part):
    shared_part = cluster_shared(key)
    noise_key = jax.random.fold_in(key, 21)
    noise_part = jnp.clip(jax.random.normal(noise_key, shared_part.shape, jnp.float32), -4.0, 4.0)
    whole = shared_part + noise_level * noise_part
    return whole.reshape(2, TOKENS, HEADS * HEAD_DIM).astype(jnp.bfloat16)


def draw_key_proj(key, part):
    shared_part = cluster_shared(key)
    noise_key = jax.random.fold_in(key, 22)
    noise_part = jnp.clip(jax.random.normal(noise_key, shared_part.shape, jnp.float32), -4.0, 4.0)
    whole = shared_part + noise_level * noise_part
    return whole.reshape(2, TOKENS, HEADS * HEAD_DIM).astype(jnp.bfloat16)


def set_ends(result, key, least, largest):
    place = [jax.random.randint(jax.random.fold_in(key, axis), (), 0, length) for axis, length in enumerate(result.shape)]
    longest = result.shape.index(max(result.shape))
    beside = place[:longest] + [(place[longest] + 1) % result.shape[longest]] + place[longest + 1:]
    return result.at[tuple(place)].set(least).at[tuple(beside)].set(largest)


def level_of(own_key, dims, shards, smallest, top_value):
    loudness = 1.0
    for axis_at, shards_of in shards:
        steps = jax.random.uniform(jax.random.fold_in(jax.random.fold_in(own_key, 6), axis_at), (shards_of,), jnp.float32, smallest / len(shards), top_value / len(shards))
        loudness = loudness * jnp.repeat(jnp.exp(steps), dims[axis_at] // shards_of).reshape((-1,) + (1,) * (len(dims) - 1 - axis_at))
    return loudness


def noise(stream_key, extent, spread, most, shards=(), kind=jnp.bfloat16):
    gain = level_of(stream_key, extent, shards, -0.22, 0.18) if shards else 1.0
    drawn = jax.random.normal(stream_key, extent, jnp.float32) * spread * gain
    return jnp.minimum(jnp.maximum(drawn, -most), most).astype(kind)


def setup_inputs(seed: int = 0) -> dict:
    streams_of = jax.random.split(jax.random.key(seed), 18)
    return {
        "hidden": noise(streams_of[0], (2, TOKENS, D), 0.5, 3.0, ((0, 2), (1, 128))),
        "queries": draw_queries(jax.random.fold_in(streams_of[17], 71), 0),
        "key_proj": draw_key_proj(jax.random.fold_in(streams_of[17], 71), 0),
        "value_proj": noise(streams_of[3], (2, TOKENS, HEADS * HEAD_DIM), 2.0, 12.0, ((0, 2), (1, 128))),
        "norm_gain": jnp.clip(1.0 + 0.18 * jax.random.normal(streams_of[4], (2, HEAD_DIM), jnp.float32), 0.1, 1.9),
        "norm_bias": noise(streams_of[5], (2, HEAD_DIM), 0.3, 2.0, (), jnp.float32),
        "positions": set_ends(jax.random.randint(streams_of[6], (3, TOKENS), 0, 48), jax.random.fold_in(streams_of[6], 1), 0, 47).astype(jnp.int32),
        "text_len": jax.random.randint(streams_of[7], (2,), 1, TEXT + 1).astype(jnp.int32),
        "time_embed": noise(streams_of[8], (TEMB,), 1.0, 6.0),
        "gate_table": noise(streams_of[9], (TEMB, D), TEMB ** -0.5, 0.25, ((1, 128),)),
        "mod_table": noise(streams_of[10], (TEMB, 2 * D), TEMB ** -0.5, 0.25, ((1, 128),)),
        "out_weight": noise(streams_of[11], (HEADS * HEAD_DIM, D), (HEADS * HEAD_DIM) ** -0.5, 0.125, ((1, 256),)),
        "proj_weight": noise(streams_of[12], (D, CHANNELS), D ** -0.5, 0.109375),
        "proj_bias": noise(streams_of[13], (CHANNELS,), 0.5, 3.0, (), jnp.float32),
        "latent": noise(streams_of[14], (TOKENS, CHANNELS), 1.0, 6.0, ((0, 128),), jnp.float32),
        "solver_coef": jnp.clip(jax.random.uniform(streams_of[15], (2, STEPS), jnp.float32, 0.3, 1.2), 0.3, 1.2),
        "step_index": jax.random.randint(streams_of[16], (1,), 0, STEPS).astype(jnp.int32),
    }


GUIDANCE = 6.0

def layer_norm(values, epsilon):
    centre = lax.optimization_barrier(jnp.mean(values, axis=-1, keepdims=True))
    centred = values - centre
    variance = lax.optimization_barrier(jnp.mean(centred * centred, axis=-1, keepdims=True))
    return centred * lax.rsqrt(variance + epsilon)

def rotary_angles(positions):
    pos_float = positions.astype(jnp.float32)
    time_freq = jnp.asarray(10000.0 ** (-2.0 * np.arange(8) / 16.0), jnp.float32)
    space_freq = jnp.asarray(10000.0 ** (-2.0 * np.arange(12) / 24.0), jnp.float32)
    return jnp.concatenate([pos_float[0][:, None] * time_freq[None, :], pos_float[1][:, None] * space_freq[None, :], pos_float[2][:, None] * space_freq[None, :]], axis=1)

def norm_rotate(values, gain_row, offset, angles, is_video):
    row_count = values.shape[0]
    head_count = values.shape[1] // 64
    normed = layer_norm(values.astype(jnp.float32).reshape(row_count, head_count, 64), 1e-06) * gain_row + offset
    paired = normed.reshape(row_count, head_count, 32, 2)
    first_half = paired[..., 0]
    second = paired[..., 1]
    cosine = jnp.cos(angles)[:, None, :]
    sine_part = jnp.sin(angles)[:, None, :]
    rotated = jnp.stack([first_half * cosine - second * sine_part, first_half * sine_part + second * cosine], axis=-1).reshape(row_count, head_count, 64)
    return jnp.where(is_video[:, None, None], rotated, normed).astype(jnp.bfloat16)

def attend_head(head_query, head_key, head_value, key_valid):
    total_rows = head_query.shape[0]
    block_rows = math.gcd(1024, total_rows)

    def one_block(query_block):
        scores = jnp.dot(query_block, head_key.T, preferred_element_type=jnp.float32) * 0.125
        weights = jnp.where(key_valid[None, :], jnp.exp(scores), 0.0)
        denominator = lax.optimization_barrier(jnp.sum(weights, axis=1, keepdims=True))
        numerator = jnp.dot(weights.astype(jnp.bfloat16), head_value, preferred_element_type=jnp.float32)
        return (numerator / denominator).astype(jnp.bfloat16)
    return lax.map(one_block, head_query.reshape(total_rows // block_rows, block_rows, 64)).reshape(total_rows, 64)

def reference(hidden, queries, key_proj, value_proj, norm_gain, norm_bias, positions, text_len, time_embed, gate_table, mod_table, out_weight, proj_weight, proj_bias, latent, solver_coef, step_index):
    row_index = jnp.arange(TOKENS)
    is_video = row_index >= TEXT_SLOTS
    angles = rotary_angles(positions)
    embed_act = jax.nn.silu(time_embed.astype(jnp.float32)).astype(jnp.bfloat16)[None, :]
    gate_vec = jnp.dot(embed_act, gate_table, preferred_element_type=jnp.float32)[0]
    modulation = jnp.dot(embed_act, mod_table, preferred_element_type=jnp.float32)[0]
    shift_part = modulation[:D]
    scale_part = modulation[D:]
    predictions = []
    for half_index in range(2):
        rot_query = norm_rotate(queries[half_index], norm_gain[0], norm_bias[0], angles, is_video)
        rot_key = norm_rotate(key_proj[half_index], norm_gain[1], norm_bias[1], angles, is_video)
        key_valid = is_video | (row_index < text_len[half_index])
        head_values = value_proj[half_index].reshape(TOKENS, HEADS, 64)

        def per_head(operands):
            return attend_head(operands[0], operands[1], operands[2], key_valid)
        attended = lax.map(per_head, (rot_query.transpose(1, 0, 2), rot_key.transpose(1, 0, 2), head_values.transpose(1, 0, 2)))
        attended = attended.transpose(1, 0, 2).reshape(TOKENS, HEADS * 64)
        projected = jnp.dot(attended, out_weight, preferred_element_type=jnp.float32)
        residual = hidden[half_index].astype(jnp.float32) + gate_vec[None, :] * projected
        normed = (layer_norm(residual, 1e-05) * (1.0 + scale_part) + shift_part).astype(jnp.bfloat16)
        predictions.append(jnp.dot(normed, proj_weight, preferred_element_type=jnp.float32) + proj_bias)
    guided = predictions[1] + GUIDANCE * (predictions[0] - predictions[1])
    step_coefs = lax.dynamic_index_in_dim(solver_coef, step_index[0], axis=1, keepdims=False)
    updated = step_coefs[0] * latent + step_coefs[1] * guided
    return jnp.where(is_video[:, None], updated, 0.0)
```

```python
import math

import jax
import jax.numpy as jnp
import numpy as np
from jax import lax
from jax.sharding import PartitionSpec as P

TEXT_SLOTS = 256


GUIDANCE = 6.0


def swapped(value, axis, bit):
    return lax.ppermute(value, axis, [(i, i ^ 1 << bit) for i in range(lax.axis_size(axis))])


def layer_norm(values, epsilon):
    centre = jnp.mean(values, axis=-1, keepdims=True)
    centred = values - centre
    variance = jnp.mean(centred * centred, axis=-1, keepdims=True)
    return centred * lax.rsqrt(variance + epsilon)


def rotary_angles(positions):
    pos_float = positions.astype(jnp.float32)
    time_freq = jnp.asarray(10000.0 ** (-2.0 * np.arange(8) / 16.0), jnp.float32)
    space_freq = jnp.asarray(10000.0 ** (-2.0 * np.arange(12) / 24.0), jnp.float32)
    return jnp.concatenate(
        [
            pos_float[0][:, None] * time_freq[None, :],
            pos_float[1][:, None] * space_freq[None, :],
            pos_float[2][:, None] * space_freq[None, :],
        ],
        axis=1,
    )


def norm_rotate(values, gain_row, offset, angles, is_video):
    row_count = values.shape[0]
    head_count = values.shape[1] // 64
    normed = (
        layer_norm(values.astype(jnp.float32).reshape(row_count, head_count, 64), 1e-06) * gain_row
        + offset
    )
    paired = normed.reshape(row_count, head_count, 32, 2)
    first_half = paired[..., 0]
    second = paired[..., 1]
    cosine = jnp.cos(angles)[:, None, :]
    sine_part = jnp.sin(angles)[:, None, :]
    rotated = jnp.stack(
        [first_half * cosine - second * sine_part, first_half * sine_part + second * cosine],
        axis=-1,
    ).reshape(row_count, head_count, 64)
    return jnp.where(is_video[:, None, None], rotated, normed).astype(jnp.bfloat16)


def on_device(
    hidden,
    queries,
    key_proj,
    value_proj,
    norm_gain,
    norm_bias,
    positions,
    text_len,
    time_embed,
    gate_table,
    mod_table,
    out_weight,
    proj_weight,
    proj_bias,
    latent,
    solver_coef,
    step_index,
):
    seq_count = lax.axis_size("seq")
    seq_place = lax.axis_index("seq")
    local_rows = queries.shape[1]
    head_count = queries.shape[2] // 64
    head_group = max(head_count // seq_count, 1)
    row_split = max(seq_count // head_count, 1)
    part_rows = local_rows // row_split
    head_sets = head_count // head_group
    row_index = seq_place * local_rows + jnp.arange(local_rows)
    is_video = row_index >= TEXT_SLOTS
    angles = rotary_angles(positions)
    rot_query = norm_rotate(queries[0], norm_gain[0], norm_bias[0], angles, is_video)
    rot_key = norm_rotate(key_proj[0], norm_gain[1], norm_bias[1], angles, is_video)
    query_send = rot_query.reshape(row_split, part_rows, head_sets, head_group, 64)
    query_send = query_send.transpose(2, 0, 1, 3, 4).reshape(seq_count, part_rows * head_group * 64)

    def spread(values):
        grouped = values.transpose(1, 0, 2)
        widened = jnp.broadcast_to(
            grouped[:, None], (head_sets, row_split, local_rows, head_group * 64)
        )
        return widened.reshape(seq_count, local_rows * head_group * 64)

    key_send = spread(rot_key)
    value_send = spread(value_proj[0].reshape(local_rows, head_count, 64))
    query_recv, key_recv, value_recv = (
        lax.all_to_all(query_send, "seq", split_axis=0, concat_axis=0, tiled=True),
        lax.all_to_all(key_send, "seq", split_axis=0, concat_axis=0, tiled=True),
        lax.all_to_all(value_send, "seq", split_axis=0, concat_axis=0, tiled=True),
    )
    total_keys = seq_count * local_rows
    query_count = seq_count * part_rows
    query_all = query_recv.reshape(query_count, head_group, 64)
    key_index = jnp.arange(total_keys)
    key_valid = (key_index >= TEXT_SLOTS) | (key_index < text_len[0])
    block_keys = math.gcd(512, total_keys)
    block_count = total_keys // block_keys

    def key_step(state_pair, operands):
        numerator, denominator = state_pair
        key_block, value_block, valid_block = operands
        scores = (
            jnp.einsum("qgd,kgd->gqk", query_all, key_block, preferred_element_type=jnp.float32)
            * 0.125
        )
        weights = jnp.where(valid_block[None, None, :], jnp.exp(scores), 0.0)
        denominator = denominator + jnp.sum(weights, axis=2)
        numerator = numerator + jnp.einsum(
            "gqk,kgd->gqd",
            weights.astype(jnp.bfloat16),
            value_block,
            preferred_element_type=jnp.float32,
        )
        return ((numerator, denominator), None)

    start_state = (
        jnp.zeros((head_group, query_count, 64), jnp.float32),
        jnp.zeros((head_group, query_count), jnp.float32),
    )
    scanned = (
        key_recv.reshape(block_count, block_keys, head_group, 64),
        value_recv.reshape(block_count, block_keys, head_group, 64),
        key_valid.reshape(block_count, block_keys),
    )
    final_state, unused_out = lax.scan(key_step, start_state, scanned)
    attended = (final_state[0] / final_state[1][..., None]).astype(jnp.bfloat16)
    back_send = attended.reshape(head_group, seq_count, part_rows, 64).transpose(1, 2, 0, 3)
    back_send = back_send.reshape(seq_count, part_rows * head_group * 64)
    back_recv = lax.all_to_all(back_send, "seq", split_axis=0, concat_axis=0, tiled=True)
    attended_rows = back_recv.reshape(head_sets, row_split, part_rows, head_group, 64)
    attended_rows = attended_rows.transpose(1, 2, 0, 3, 4).reshape(local_rows, head_count * 64)
    embed_act = jax.nn.silu(time_embed.astype(jnp.float32)).astype(jnp.bfloat16)[None, :]
    gate_own = jnp.dot(embed_act, gate_table, preferred_element_type=jnp.float32)
    mod_own = jnp.dot(embed_act, mod_table, preferred_element_type=jnp.float32)
    own_vec = jnp.concatenate([gate_own, mod_own], axis=1)
    gate_width = gate_own.shape[1]
    all_vec = lax.all_to_all(
        jnp.broadcast_to(own_vec, (seq_count, own_vec.shape[1])),
        "seq", split_axis=0, concat_axis=0, tiled=True,
    )
    gate_vec = all_vec[:, :gate_width].reshape(-1)
    modulation = all_vec[:, gate_width:].reshape(-1)
    projected = jnp.dot(
        attended_rows,
        lax.all_gather(out_weight, ("cfg", "seq"), axis=1, tiled=True),
        preferred_element_type=jnp.float32,
    )
    model_width = hidden.shape[2]
    residual = hidden[0].astype(jnp.float32) + gate_vec[None, :] * projected
    normed = (
        layer_norm(residual, 1e-05) * (1.0 + modulation[model_width:]) + modulation[:model_width]
    )
    normed = normed.astype(jnp.bfloat16)
    prediction = jnp.dot(normed, proj_weight, preferred_element_type=jnp.float32) + proj_bias
    cfg_place = lax.axis_index("cfg")
    own_width = prediction.shape[1] // 2
    own_pred = lax.dynamic_slice_in_dim(prediction, cfg_place * own_width, own_width, 1)
    sent_pred = lax.dynamic_slice_in_dim(prediction, (1 - cfg_place) * own_width, own_width, 1)
    partner = swapped(sent_pred, "cfg", 0)
    is_cond = cfg_place == 0
    cond_pred = jnp.where(is_cond, own_pred, partner)
    uncond_pred = jnp.where(is_cond, partner, own_pred)
    guided = uncond_pred + GUIDANCE * (cond_pred - uncond_pred)
    own_latent = lax.dynamic_slice_in_dim(latent, cfg_place * own_width, own_width, 1)
    step_coefs = lax.dynamic_index_in_dim(solver_coef, step_index[0], axis=1, keepdims=False)
    updated = step_coefs[0] * own_latent + step_coefs[1] * guided
    return jnp.where(is_video[:, None], updated, 0.0)


def solution(mesh):
    placed = (
        P("cfg", "seq", None),
        P("cfg", "seq", None),
        P("cfg", "seq", None),
        P("cfg", "seq", None),
        P(),
        P(),
        P(None, "seq"),
        P("cfg"),
        P(),
        P(None, "seq"),
        P(None, "seq"),
        P(None, ("cfg", "seq")),
        P(),
        P(),
        P("seq", None),
        P(),
        P(),
    )
    return jax.shard_map(
        on_device, mesh=mesh, in_specs=placed, out_specs=P("seq", "cfg"), check_vma=False
    )
```

```python
import functools

import jax
import jax.numpy as jnp
import numpy as np
from jax import lax
from jax.experimental import pallas as pl
from jax.experimental.pallas import tpu as pltpu
from jax.sharding import PartitionSpec as P

TEXT_SLOTS = 256
GUIDANCE = 6.0
HALF = 64
MIB = 1 << 20
F32 = jnp.float32
BF16 = jnp.bfloat16
NT = (((1,), (1,)), ((), ()))


def lane_iota(shape):
    return lax.broadcasted_iota(jnp.int32, shape, len(shape) - 1)


def vmem(n):
    return [pl.BlockSpec(memory_space=pltpu.VMEM)] * n


def smem(n):
    return [pl.BlockSpec(memory_space=pltpu.SMEM)] * n


def normed(stacked, gain, bias, ones):
    mean = jnp.dot(stacked.astype(BF16), ones.astype(BF16), preferred_element_type=F32) * (1.0 / 64)
    centred = stacked - mean
    var = jnp.dot(
        centred * centred, ones, preferred_element_type=F32, precision=lax.Precision.HIGHEST
    ) * (1.0 / 64)
    return centred * lax.rsqrt(var + 1e-6) * gain + bias


def rotated(values, cosine, sine):
    lane = lane_iota(values.shape)
    other = jnp.where(lane % 2 == 0, pltpu.roll(values, 127, 1), pltpu.roll(values, 1, 1))
    return (values * cosine + other * sine).astype(BF16).astype(F32)


def prologue_kernel(
    scal, q_ref, k_ref, v_ref, cos_ref, sin_ref, gain_ref, bias_ref, emb_ref, gate_ref, mod_ref,
    send_ref, table,
):
    rows = q_ref.shape[0]
    blocks = q_ref.shape[1] // 128
    r = lax.broadcasted_iota(jnp.int32, (128, 128), 0)
    c = lax.broadcasted_iota(jnp.int32, (128, 128), 1)
    ones = jnp.where((r < HALF) == (c < HALF), 1.0, 0.0).astype(F32)
    cosine = jnp.concatenate([cos_ref[...]] * blocks, axis=0)
    sine = jnp.concatenate([sin_ref[...]] * blocks, axis=0)

    def stack(ref):
        x = ref[...].astype(F32)
        return jnp.concatenate([x[:, 128 * p : 128 * p + 128] for p in range(blocks)], axis=0)

    q_all = rotated(normed(stack(q_ref), gain_ref[0:1], bias_ref[0:1], ones), cosine, sine) * 0.125
    k_all = rotated(normed(stack(k_ref), gain_ref[1:2], bias_ref[1:2], ones), cosine, sine)
    token = scal[0] + lax.broadcasted_iota(jnp.int32, (rows, 128), 0)
    valid = (token >= TEXT_SLOTS) | (token < scal[1])
    lane = lane_iota((rows, 128))

    emb = emb_ref[...].astype(F32)
    act = (emb / (1.0 + jnp.exp(-emb))).astype(BF16)
    act = jnp.broadcast_to(act, (8, act.shape[1]))
    table[...] = jnp.zeros_like(table)
    table[0, HALF : HALF + mod_ref.shape[0]] = mod_ref[...]
    table[1, HALF : HALF + gate_ref.shape[0]] = gate_ref[...]
    row8 = lax.broadcasted_iota(jnp.int32, (8, 128), 0)
    extra = jnp.zeros((8, 128), F32)
    for t in range(2):
        rest = lax.dot_general(act, table[t], NT, preferred_element_type=F32)
        for part in range(3):
            term = rest.astype(BF16).astype(F32)
            extra = jnp.where(row8 == 3 * t + part, term, extra)
            rest = rest - term

    lane16 = lane_iota((16, 128))
    for p in range(blocks):
        qb = q_all[rows * p : rows * (p + 1)]
        kb = jnp.where(valid, k_all[rows * p : rows * (p + 1)], 0.0)
        vb = jnp.where(valid, v_ref[:, 128 * p : 128 * p + 128].astype(F32), 0.0)
        qr, kr, vr = (pltpu.roll(t, HALF, 1) for t in (qb, kb, vb))
        for odd in range(2):
            kv = jnp.where(lane < HALF, kr, vb) if odd else jnp.where(lane < HALF, kb, vr)
            low, high = (qr, qb) if odd else (qb, qr)
            for part in range(2):
                dest = 2 * (2 * p + odd) + part
                at = 24 * part
                send_ref[dest, 0:24] = kv[at : at + 24].astype(BF16)
                upper = jnp.concatenate([high[at + 16 : at + 24], extra], axis=0)
                send_ref[dest, 24:40] = jnp.where(lane16 < HALF, low[at : at + 16], upper).astype(BF16)


def unpack_kernel(recv_ref, kv_ref, q_ref):
    n = recv_ref.shape[0]
    kv_ref[...] = recv_ref[:, 0:24, :]
    low = recv_ref[:, 24:40, :].astype(F32).reshape(n * 16, 128)
    q_ref[0 : n * 16] = jnp.where(lane_iota(low.shape) < HALF, low, 0.0).astype(BF16)
    high = pltpu.roll(recv_ref[:, 24:32, :].astype(F32).reshape(n * 8, 128), HALF, 1)
    q_ref[n * 16 : n * 24] = jnp.where(lane_iota(high.shape) < HALF, high, 0.0).astype(BF16)


def attend_kernel(first, last, scal, q_ref, kv_ref, *rest):
    acc_in = None if first else rest[0]
    rest = rest if first else rest[1:]
    out_ref, va = rest[0], rest[1]
    acc = rest[2] if last else out_ref
    keys = kv_ref.shape[0]
    queries = q_ref.shape[0]
    lane = lane_iota((256, 128))
    n = lax.broadcasted_iota(jnp.int32, (256, 128), 0).astype(F32)
    source = jnp.floor((n + 0.5) * (1.0 / 24))
    token = (scal[0] * 64).astype(F32) * 48 + source * 48 + (scal[1] * 24).astype(F32) + (n - source * 24)
    valid = (token >= TEXT_SLOTS) | (token < scal[2].astype(F32))
    va[0:256] = jnp.where(lane < HALF, jnp.where(valid, 1.0, 0.0), kv_ref[0:256].astype(F32)).astype(BF16)
    big = lane_iota((keys - 256, 128))
    va[256:] = jnp.where(big < HALF, 1.0, kv_ref[256:].astype(F32)).astype(BF16)
    q_step, k_step = 256, 512

    def block(i, carry):
        at = pl.ds(pl.multiple_of(i * q_step, q_step), q_step)
        q = q_ref[at, :]
        total = None if first else acc_in[at, :]
        for k0 in range(0, keys, k_step):
            s = lax.dot_general(q, kv_ref[k0 : k0 + k_step], NT, preferred_element_type=F32)
            p = jnp.exp(s).astype(BF16)
            part = jnp.dot(p, va[k0 : k0 + k_step], preferred_element_type=F32)
            total = part if total is None else total + part
        acc[at, :] = total
        return carry

    lax.fori_loop(0, queries // q_step, block, 0)
    if last:
        n_src = out_ref.shape[0]

        def ratio(x):
            return x / pltpu.roll(x, HALF, 1)

        for base, size, to in ((0, 16, 0), (n_src * 16, 8, 16)):
            x = ratio(acc[base : base + n_src * size, :])
            back = pltpu.roll(x, HALF, 1).reshape(n_src // 2, 2, size, 128)
            x = x.reshape(n_src // 2, 2, size, 128)
            both = jnp.where(lane_iota((n_src // 2, size, 128)) < HALF, back[:, 0], x[:, 1])
            both = both.astype(BF16)
            for chip in range(n_src // 2):
                out_ref[2 * chip, to : to + size] = both[chip]
                out_ref[2 * chip + 1, to : to + size] = both[chip]


def attend(scal, q, kv, acc, last):
    first = acc is None
    keys, queries = kv.shape[0], q.shape[0]
    n_src = keys // 24
    out = jax.ShapeDtypeStruct((n_src, 24, 128), BF16) if last else jax.ShapeDtypeStruct((queries, 128), F32)
    scratch = [pltpu.VMEM((keys, 128), BF16)]
    if last:
        scratch.append(pltpu.VMEM((queries, 128), F32))
    args = (scal, q, kv) if first else (scal, q, kv, acc)
    return pl.pallas_call(
        functools.partial(attend_kernel, first, last),
        out_shape=out,
        in_specs=smem(1) + vmem(len(args) - 1),
        out_specs=pl.BlockSpec(memory_space=pltpu.VMEM),
        scratch_shapes=scratch,
        cost_estimate=pl.CostEstimate(
            flops=4 * keys * queries * 256, transcendentals=keys * queries, bytes_accessed=2 * MIB
        ),
        compiler_params=pltpu.CompilerParams(vmem_limit_bytes=24 * MIB),
        name="attend",
    )(*args)


def project_kernel(scal, recv_ref, *rest):
    pieces, (own_ref, other_ref, att, total, natural) = rest[:8], rest[8:]
    core, ring_y, ring_x, ring_z = scal[0], scal[1], scal[2], scal[3]
    heads = recv_ref.shape[0] // 4
    base = core * (2 * heads)
    lane = lane_iota((24, 128))
    att[96:128] = jnp.zeros((32, att.shape[1]), BF16)
    for m in range(heads // 2):
        for part in range(2):
            a = recv_ref[base + 4 * m + part].astype(F32)
            b = recv_ref[base + 4 * m + 2 + part].astype(F32)
            cols = slice(128 * m, 128 * m + 128)
            att[24 * part : 24 * part + 24, cols] = jnp.where(lane < HALF, a, pltpu.roll(b, HALF, 1)).astype(BF16)
            att[48 + 24 * part : 72 + 24 * part, cols] = jnp.where(lane < HALF, pltpu.roll(a, HALF, 1), b).astype(BF16)
    quarter = att.shape[1] // 2
    for colour in range(2):
        rhs = att[:, colour * quarter : (colour + 1) * quarter]
        for far in range(4):
            ref = pieces[4 * colour + far]
            for near in range(4):
                dy, dx = (far, near) if colour == 0 else (near, far)
                y = lax.rem(ring_y - dy + 4, 4)
                x = lax.rem(ring_x - dx + 4, 4)
                res = lax.dot_general(ref[192 * near : 192 * near + 192], rhs, NT, preferred_element_type=F32)
                for dz in range(8):
                    z = lax.rem(ring_z - dz + 8, 8)
                    at = pl.ds(pl.multiple_of((y * 32 + x * 8 + z) * 24, 8), 24)
                    part = res[24 * dz : 24 * dz + 24]
                    total[at, :] = part if colour == 0 else total[at, :] + part
    for b in range(total.shape[0] // 128):
        natural[:, 128 * b : 128 * b + 128] = total[128 * b : 128 * b + 128, :].T
    own_ref[...] = natural[pl.ds(pl.multiple_of(core * 48, 8), 48), :]
    other_ref[...] = natural[pl.ds(pl.multiple_of((1 - core) * 48, 8), 48), :]


def final_kernel(own, other, hidden, gate, shift, scale, weight, bias, out):
    x = hidden[...].astype(F32) + gate[...] * (own[...] + other[...])
    centred = x - jnp.mean(x, axis=1, keepdims=True)
    var = jnp.mean(centred * centred, axis=1, keepdims=True)
    y = centred * lax.rsqrt(var + 1e-5) * (1.0 + scale[...]) + shift[...]
    out[...] = jnp.dot(y.astype(BF16), weight[...], preferred_element_type=F32) + bias[...]


def on_device(
    hidden, queries, key_proj, value_proj, norm_gain, norm_bias, positions, text_len, time_embed,
    gate_table, mod_table, out_weight, proj_weight, proj_bias, latent, solver_coef, step_index,
):
    both = ("cfg", "seq")
    seq_count = lax.axis_size("seq")
    cfg_place, place = lax.axis_index("cfg"), lax.axis_index("seq")
    core, z, x, y = place % 2, place // 2 % 8, place // 16 % 4, place // 64
    ring_y = cfg_place * 2 + y
    rows = queries.shape[1]

    def send(value, dx=0, dy=0, dz=0, dc=0):
        pairs = []
        for i in range(2 * seq_count):
            c_, z_, x_, y_ = i % 2, i // 2 % 8, i // 16 % 4, i // 64
            target = (y_ + dy) % 4 * 64 + (x_ + dx) % 4 * 16 + (z_ + dz) % 8 * 2 + (c_ + dc) % 2
            pairs.append((i, target))
        return lax.ppermute(value, both, pairs)

    with jax.named_scope("weights"):
        columns = out_weight.T
        depth = columns.shape[1] // 2
        mine = lax.dynamic_slice_in_dim(columns, core * depth, depth, 1)
        theirs = send(lax.dynamic_slice_in_dim(columns, (1 - core) * depth, depth, 1), dc=1)
        block = jnp.where(
            core == 0, jnp.concatenate([mine, theirs], 0), jnp.concatenate([theirs, mine], 0)
        )
        along_z = jnp.concatenate([block] + [send(block, dz=d) for d in range(1, 8)], 0)
        first, second = along_z[:, : depth // 2], along_z[:, depth // 2 :]
        near_a = jnp.concatenate([first] + [send(first, dx=d) for d in range(1, 4)], 0)
        near_b = jnp.concatenate([second] + [send(second, dy=d) for d in range(1, 4)], 0)
        pieces = [near_a] + [send(near_a, dy=d) for d in range(1, 4)]
        pieces += [near_b] + [send(near_b, dx=d) for d in range(1, 4)]

    pair = np.arange(128) % 64 // 2
    index = np.where(pair < 8, pair, np.where(pair < 20, pair - 8, pair - 20))
    width = np.where(pair < 8, 16.0, 24.0)
    freq = jnp.asarray(10000.0 ** (-2.0 * index / width), F32)[None, :]
    pos = positions.astype(F32)[:, :, None]
    angle = jnp.where((pair < 8)[None], pos[0], jnp.where((pair < 20)[None], pos[1], pos[2])) * freq
    is_video = (place * rows + jnp.arange(rows) >= TEXT_SLOTS)[:, None]
    cosine = jnp.where(is_video, jnp.cos(angle), 1.0)
    sign = jnp.asarray(np.where(np.arange(128) % 2 == 0, -1.0, 1.0), F32)[None, :]
    sine = jnp.where(is_video, jnp.sin(angle) * sign, 0.0)
    own_scal = jnp.stack([place * rows, text_len[0]]).astype(jnp.int32)
    message = pl.pallas_call(
        prologue_kernel,
        out_shape=jax.ShapeDtypeStruct((64, 40, 128), BF16),
        in_specs=smem(1) + vmem(10),
        out_specs=pl.BlockSpec(memory_space=pltpu.VMEM),
        scratch_shapes=[pltpu.VMEM((2, 128, time_embed.shape[0]), BF16)],
        compiler_params=pltpu.CompilerParams(vmem_limit_bytes=32 * MIB),
        cost_estimate=pl.CostEstimate(flops=10**9, transcendentals=10**5, bytes_accessed=2 * MIB),
        name="prologue",
    )(
        own_scal, queries[0], key_proj[0], value_proj[0], cosine, sine,
        jnp.tile(norm_gain, (1, 2)), jnp.tile(norm_bias, (1, 2)), time_embed[None, :],
        gate_table.T, mod_table.T,
    )
    planes = [list(range(64)), list(range(64, 128))]
    received = lax.all_to_all(
        message, "seq", split_axis=0, concat_axis=0, tiled=True, axis_index_groups=planes
    )
    kv_own, q = pl.pallas_call(
        unpack_kernel,
        out_shape=(jax.ShapeDtypeStruct((64, 24, 128), BF16), jax.ShapeDtypeStruct((1536, 128), BF16)),
        in_specs=vmem(1),
        out_specs=tuple(vmem(2)),
        compiler_params=pltpu.CompilerParams(vmem_limit_bytes=16 * MIB),
        cost_estimate=pl.CostEstimate(flops=10**6, transcendentals=0, bytes_accessed=2 * MIB),
        name="unpack",
    )(received)
    kv_own = kv_own.reshape(1536, 128)
    flip_y = [(i, i ^ 64) for i in range(seq_count)]
    flip_core = [(i, i ^ 1) for i in range(seq_count)]
    kv_y = lax.ppermute(kv_own, "seq", flip_y)
    kv_core = lax.ppermute(kv_own, "seq", flip_core)
    kv_far = lax.ppermute(kv_y, "seq", flip_core)

    terms = received[:, 32:38, HALF : HALF + 48]
    terms_y = lax.ppermute(terms, "seq", flip_y)

    def scal_of(plane, part):
        return jnp.stack([plane, part, text_len[0]]).astype(jnp.int32)

    acc = attend(scal_of(y, core), q, kv_own, None, False)
    acc = attend(scal_of(y, 1 - core), q, kv_core, acc, False)
    acc = attend(scal_of(1 - y, core), q, kv_y, acc, False)
    answer = attend(scal_of(1 - y, 1 - core), q, kv_far, acc, True)
    returned = lax.all_to_all(
        answer, "seq", split_axis=0, concat_axis=0, tiled=True, axis_index_groups=planes
    )

    model_width = hidden.shape[2]
    terms = jnp.where(y == 0, jnp.stack([terms, terms_y]), jnp.stack([terms_y, terms]))
    terms = terms.astype(F32).reshape(seq_count, 2, 3, 48)
    vectors = terms[:, :, 0] + terms[:, :, 1] + terms[:, :, 2]
    modulation = vectors[:, 0].reshape(2, model_width)
    gate_vec = vectors[:, 1, :24].reshape(1, model_width)

    place_scal = jnp.stack([core, ring_y, x, z]).astype(jnp.int32)
    own_part, other_part = pl.pallas_call(
        project_kernel,
        out_shape=(jax.ShapeDtypeStruct((rows, model_width), F32),) * 2,
        in_specs=smem(1) + vmem(9),
        out_specs=tuple(vmem(2)),
        scratch_shapes=[
            pltpu.VMEM((128, depth), BF16),
            pltpu.VMEM((model_width, 128), F32),
            pltpu.VMEM((128, model_width), F32),
        ],
        compiler_params=pltpu.CompilerParams(vmem_limit_bytes=32 * MIB),
        cost_estimate=pl.CostEstimate(flops=10**9, transcendentals=0, bytes_accessed=8 * MIB),
        name="project",
    )(place_scal, returned, *pieces)
    got_part = lax.ppermute(other_part, "seq", flip_core)
    prediction = pl.pallas_call(
        final_kernel,
        out_shape=jax.ShapeDtypeStruct((rows, proj_weight.shape[1]), F32),
        in_specs=vmem(8),
        out_specs=pl.BlockSpec(memory_space=pltpu.VMEM),
        compiler_params=pltpu.CompilerParams(vmem_limit_bytes=24 * MIB),
        cost_estimate=pl.CostEstimate(flops=10**8, transcendentals=0, bytes_accessed=2 * MIB),
        name="finish",
    )(
        own_part, got_part, hidden[0], gate_vec, modulation[0:1], modulation[1:2], proj_weight,
        proj_bias[None, :],
    )
    own_width = prediction.shape[1] // 2
    own_pred = lax.dynamic_slice_in_dim(prediction, cfg_place * own_width, own_width, 1)
    sent_pred = lax.dynamic_slice_in_dim(prediction, (1 - cfg_place) * own_width, own_width, 1)
    partner = lax.ppermute(sent_pred, "cfg", [(0, 1), (1, 0)])
    is_cond = cfg_place == 0
    cond_pred = jnp.where(is_cond, own_pred, partner)
    uncond_pred = jnp.where(is_cond, partner, own_pred)
    guided = uncond_pred + GUIDANCE * (cond_pred - uncond_pred)
    own_latent = lax.dynamic_slice_in_dim(latent, cfg_place * own_width, own_width, 1)
    step_coefs = lax.dynamic_index_in_dim(solver_coef, step_index[0], axis=1, keepdims=False)
    updated = step_coefs[0] * own_latent + step_coefs[1] * guided
    return jnp.where(is_video, updated, 0.0)


def solution(mesh):
    placed = (
        P("cfg", "seq", None), P("cfg", "seq", None), P("cfg", "seq", None), P("cfg", "seq", None),
        P(), P(), P(None, "seq"), P("cfg"), P(), P(None, "seq"), P(None, "seq"), P(None, ("cfg", "seq")),
        P(), P(), P("seq", None), P(), P(),
    )
    return jax.shard_map(
        on_device, mesh=mesh, in_specs=placed, out_specs=P("seq", "cfg"), check_vma=False
    )
```

```python
import functools

import jax
import jax.numpy as jnp
import numpy as np
from jax import lax
from jax.experimental import pallas as pl
from jax.experimental.pallas import tpu as pltpu
from jax.sharding import PartitionSpec as P

TEXT_SLOTS = 256
GUIDANCE = 6.0
HALF = 64
MIB = 1 << 20
F32 = jnp.float32
BF16 = jnp.bfloat16
NT = (((1,), (1,)), ((), ()))


def lane_iota(shape):
    return lax.broadcasted_iota(jnp.int32, shape, len(shape) - 1)


def vmem(n):
    return [pl.BlockSpec(memory_space=pltpu.VMEM)] * n


def smem(n):
    return [pl.BlockSpec(memory_space=pltpu.SMEM)] * n


def normed(stacked, gain, bias, ones):
    mean = jnp.dot(stacked.astype(BF16), ones.astype(BF16), preferred_element_type=F32) * (1.0 / 64)
    centred = stacked - mean
    var = jnp.dot(
        centred * centred, ones, preferred_element_type=F32, precision=lax.Precision.HIGHEST
    ) * (1.0 / 64)
    return centred * lax.rsqrt(var + 1e-6) * gain + bias


def rotated(values, cosine, sine):
    lane = lane_iota(values.shape)
    other = jnp.where(lane % 2 == 0, pltpu.roll(values, 127, 1), pltpu.roll(values, 1, 1))
    return (values * cosine + other * sine).astype(BF16).astype(F32)


def prologue_kernel(
    scal, q_ref, k_ref, v_ref, cos_ref, sin_ref, gain_ref, bias_ref, emb_ref, gate_ref, mod_ref,
    send_ref, table,
):
    rows = q_ref.shape[0]
    blocks = q_ref.shape[1] // 128
    gain = jnp.concatenate([gain_ref[...]] * 2, axis=1)
    bias = jnp.concatenate([bias_ref[...]] * 2, axis=1)
    r = lax.broadcasted_iota(jnp.int32, (128, 128), 0)
    c = lax.broadcasted_iota(jnp.int32, (128, 128), 1)
    ones = jnp.where((r < HALF) == (c < HALF), 1.0, 0.0).astype(F32)
    cosine = jnp.concatenate([cos_ref[...]] * blocks, axis=0)
    sine = jnp.concatenate([sin_ref[...]] * blocks, axis=0)

    def stack(ref):
        x = ref[...].astype(F32)
        return jnp.concatenate([x[:, 128 * p : 128 * p + 128] for p in range(blocks)], axis=0)

    q_all = rotated(normed(stack(q_ref), gain[0:1], bias[0:1], ones), cosine, sine) * 0.125
    k_all = rotated(normed(stack(k_ref), gain[1:2], bias[1:2], ones), cosine, sine)
    token = scal[0] + lax.broadcasted_iota(jnp.int32, (rows, 128), 0)
    valid = (token >= TEXT_SLOTS) | (token < scal[1])
    lane = lane_iota((rows, 128))

    emb = emb_ref[...].astype(F32)
    act = emb / (1.0 + jnp.exp(-emb))
    table[...] = jnp.zeros_like(table)
    table[0, HALF : HALF + mod_ref.shape[0]] = mod_ref[...]
    table[1, HALF : HALF + gate_ref.shape[0]] = gate_ref[...]
    row8 = lax.broadcasted_iota(jnp.int32, (8, 128), 0)
    extra = jnp.zeros((8, 128), F32)
    for t in range(2):
        rest = jnp.zeros((8, 128), F32)
        for k in range(act.shape[0]):
            part = jnp.broadcast_to(act[k : k + 1], (8, 128)).astype(BF16)
            rest += lax.dot_general(part, table[t, :, 128 * k : 128 * k + 128], NT, preferred_element_type=F32)
        for part in range(3):
            term = rest.astype(BF16).astype(F32)
            extra = jnp.where(row8 == 3 * t + part, term, extra)
            rest = rest - term

    lane16 = lane_iota((16, 128))
    for p in range(blocks):
        qb = q_all[rows * p : rows * (p + 1)]
        kb = jnp.where(valid, k_all[rows * p : rows * (p + 1)], 0.0)
        vb = jnp.where(valid, v_ref[:, 128 * p : 128 * p + 128].astype(F32), 0.0)
        qr, kr, vr = (pltpu.roll(t, HALF, 1) for t in (qb, kb, vb))
        for odd in range(2):
            kv = jnp.where(lane < HALF, kr, vb) if odd else jnp.where(lane < HALF, kb, vr)
            low, high = (qr, qb) if odd else (qb, qr)
            for part in range(2):
                dest = 2 * (2 * p + odd) + part
                at = 24 * part
                send_ref[dest, 0:24] = kv[at : at + 24].astype(BF16)
                upper = jnp.concatenate([high[at + 16 : at + 24], extra], axis=0)
                send_ref[dest, 24:40] = jnp.where(lane16 < HALF, low[at : at + 16], upper).astype(BF16)


def unpack_kernel(recv_ref, kv_ref, q_ref):
    n = recv_ref.shape[0]
    kv_ref[...] = recv_ref[:, 0:24, :]
    low = recv_ref[:, 24:40, :].astype(F32).reshape(n * 16, 128)
    q_ref[0 : n * 16] = jnp.where(lane_iota(low.shape) < HALF, low, 0.0).astype(BF16)
    high = pltpu.roll(recv_ref[:, 24:32, :].astype(F32).reshape(n * 8, 128), HALF, 1)
    q_ref[n * 16 : n * 24] = jnp.where(lane_iota(high.shape) < HALF, high, 0.0).astype(BF16)


def attend_kernel(first, last, scal, q_ref, kv_ref, *rest):
    acc_in = None if first else rest[0]
    rest = rest if first else rest[1:]
    out_ref, va = rest[0], rest[1]
    acc = rest[2] if last else out_ref
    keys = kv_ref.shape[0]
    queries = q_ref.shape[0]
    lane = lane_iota((256, 128))
    n = lax.broadcasted_iota(jnp.int32, (256, 128), 0).astype(F32)
    source = jnp.floor((n + 0.5) * (1.0 / 24))
    token = (scal[0] * 64).astype(F32) * 48 + source * 48 + (scal[1] * 24).astype(F32) + (n - source * 24)
    valid = (token >= TEXT_SLOTS) | (token < scal[2].astype(F32))
    va[0:256] = jnp.where(lane < HALF, jnp.where(valid, 1.0, 0.0), kv_ref[0:256].astype(F32)).astype(BF16)
    big = lane_iota((keys - 256, 128))
    va[256:] = jnp.where(big < HALF, 1.0, kv_ref[256:].astype(F32)).astype(BF16)
    q_step, k_step = 256, 512

    def block(i, carry):
        at = pl.ds(pl.multiple_of(i * q_step, q_step), q_step)
        q = q_ref[at, :]
        total = None if first else acc_in[at, :]
        for k0 in range(0, keys, k_step):
            s = lax.dot_general(q, kv_ref[k0 : k0 + k_step], NT, preferred_element_type=F32)
            p = jnp.exp(s).astype(BF16)
            part = jnp.dot(p, va[k0 : k0 + k_step], preferred_element_type=F32)
            total = part if total is None else total + part
        acc[at, :] = total
        return carry

    lax.fori_loop(0, queries // q_step, block, 0)
    if last:
        n_src = out_ref.shape[0]

        def ratio(x):
            return x / pltpu.roll(x, HALF, 1)

        for base, size, to in ((0, 16, 0), (n_src * 16, 8, 16)):
            x = ratio(acc[base : base + n_src * size, :])
            back = pltpu.roll(x, HALF, 1).reshape(n_src // 2, 2, size, 128)
            x = x.reshape(n_src // 2, 2, size, 128)
            both = jnp.where(lane_iota((n_src // 2, size, 128)) < HALF, back[:, 0], x[:, 1])
            both = both.astype(BF16)
            for chip in range(n_src // 2):
                out_ref[2 * chip, to : to + size] = both[chip]
                out_ref[2 * chip + 1, to : to + size] = both[chip]


def attend(scal, q, kv, acc, last):
    first = acc is None
    keys, queries = kv.shape[0], q.shape[0]
    n_src = keys // 24
    out = jax.ShapeDtypeStruct((n_src, 24, 128), BF16) if last else jax.ShapeDtypeStruct((queries, 128), F32)
    scratch = [pltpu.VMEM((keys, 128), BF16)]
    if last:
        scratch.append(pltpu.VMEM((queries, 128), F32))
    args = (scal, q, kv) if first else (scal, q, kv, acc)
    return pl.pallas_call(
        functools.partial(attend_kernel, first, last),
        out_shape=out,
        in_specs=smem(1) + vmem(len(args) - 1),
        out_specs=pl.BlockSpec(memory_space=pltpu.VMEM),
        scratch_shapes=scratch,
        cost_estimate=pl.CostEstimate(
            flops=4 * keys * queries * 256, transcendentals=keys * queries, bytes_accessed=2 * MIB
        ),
        compiler_params=pltpu.CompilerParams(vmem_limit_bytes=24 * MIB),
        name="attend",
    )(*args)


def project_kernel(scal, recv_ref, *rest):
    pieces, (own_ref, other_ref, att, total, natural) = rest[:8], rest[8:]
    core, ring_y, ring_x = scal[0], scal[1], scal[2]
    heads = recv_ref.shape[0] // 4
    base = core * (2 * heads)
    lane = lane_iota((24, 128))
    att[96:128] = jnp.zeros((32, att.shape[1]), BF16)
    for m in range(heads // 2):
        for part in range(2):
            a = recv_ref[base + 4 * m + part].astype(F32)
            b = recv_ref[base + 4 * m + 2 + part].astype(F32)
            cols = slice(128 * m, 128 * m + 128)
            att[24 * part : 24 * part + 24, cols] = jnp.where(lane < HALF, a, pltpu.roll(b, HALF, 1)).astype(BF16)
            att[48 + 24 * part : 72 + 24 * part, cols] = jnp.where(lane < HALF, pltpu.roll(a, HALF, 1), b).astype(BF16)
    quarter = att.shape[1] // 2
    for colour in range(2):
        rhs = att[:, colour * quarter : (colour + 1) * quarter]
        for far in range(4):
            ref = pieces[4 * colour + far]
            for near in range(4):
                dy, dx = (far, near) if colour == 0 else (near, far)
                y = lax.rem(ring_y - dy + 4, 4)
                x = lax.rem(ring_x - dx + 4, 4)
                res = lax.dot_general(ref[192 * near : 192 * near + 192], rhs, NT, preferred_element_type=F32)
                at = pl.ds(pl.multiple_of((y * 4 + x) * 192, 192), 192)
                total[at, :] = res if colour == 0 else total[at, :] + res
    for b in range(total.shape[0] // 128):
        natural[:, 128 * b : 128 * b + 128] = total[128 * b : 128 * b + 128, :].T
    own_ref[...] = natural[pl.ds(pl.multiple_of(core * 48, 8), 48), :]
    other_ref[...] = natural[pl.ds(pl.multiple_of((1 - core) * 48, 8), 48), :]


def final_kernel(cfg, own, other, hidden, gate, shift, scale, weight, bias, out, sent, both):
    x = hidden[...].astype(F32) + gate[...] * (own[...] + other[...])
    centred = x - jnp.mean(x, axis=1, keepdims=True)
    var = jnp.mean(centred * centred, axis=1, keepdims=True)
    y = centred * lax.rsqrt(var + 1e-5) * (1.0 + scale[...]) + shift[...]
    both[...] = lax.dot_general(weight[...], y.astype(BF16), NT, preferred_element_type=F32) + bias[...]
    width = out.shape[0]
    out[...] = both[pl.ds(pl.multiple_of(cfg[0] * width, 8), width), :]
    sent[...] = both[pl.ds(pl.multiple_of((1 - cfg[0]) * width, 8), width), :]


def on_device(
    hidden, queries, key_proj, value_proj, norm_gain, norm_bias, positions, text_len, time_embed,
    gate_table, mod_table, out_weight, proj_weight, proj_bias, latent, solver_coef, step_index,
):
    both = ("cfg", "seq")
    seq_count = lax.axis_size("seq")
    cfg_place, place = lax.axis_index("cfg"), lax.axis_index("seq")
    core, z, x, y = place % 2, place // 2 % 8, place // 16 % 4, place // 64
    ring_y = cfg_place * 2 + y
    rows = queries.shape[1]

    def send(value, dx=0, dy=0, dz=0, dc=0):
        pairs = []
        for i in range(2 * seq_count):
            c_, z_, x_, y_ = i % 2, i // 2 % 8, i // 16 % 4, i // 64
            target = (y_ + dy) % 4 * 64 + (x_ + dx) % 4 * 16 + (z_ + dz) % 8 * 2 + (c_ + dc) % 2
            pairs.append((i, target))
        return lax.ppermute(value, both, pairs)

    with jax.named_scope("weights"):
        columns = out_weight.T
        width, depth = columns.shape[0], columns.shape[1] // 2
        halves = columns.reshape(width, 2, depth).transpose(1, 0, 2)
        shares = jnp.broadcast_to(halves[None], (8, 2, width, depth)).reshape(16, width, depth)
        rings = [list(range(i, i + 16)) for i in range(0, seq_count, 16)]
        along_z = lax.all_to_all(
            shares, "seq", split_axis=0, concat_axis=0, tiled=True, axis_index_groups=rings
        ).reshape(16 * width, depth)
        first, second = along_z[:, : depth // 2], along_z[:, depth // 2 :]

    pair = np.arange(128) % 64 // 2
    index = np.where(pair < 8, pair, np.where(pair < 20, pair - 8, pair - 20))
    width = np.where(pair < 8, 16.0, 24.0)
    freq = jnp.asarray(10000.0 ** (-2.0 * index / width), F32)[None, :]
    pos = positions.astype(F32)[:, :, None]
    angle = jnp.where((pair < 8)[None], pos[0], jnp.where((pair < 20)[None], pos[1], pos[2])) * freq
    is_video = (place * rows + jnp.arange(rows) >= TEXT_SLOTS)[:, None]
    cosine = jnp.where(is_video, jnp.cos(angle), 1.0)
    sign = jnp.asarray(np.where(np.arange(128) % 2 == 0, -1.0, 1.0), F32)[None, :]
    sine = jnp.where(is_video, jnp.sin(angle) * sign, 0.0)
    own_scal = jnp.stack([place * rows, text_len[0]]).astype(jnp.int32)
    message = pl.pallas_call(
        prologue_kernel,
        out_shape=jax.ShapeDtypeStruct((64, 40, 128), BF16),
        in_specs=smem(1) + vmem(10),
        out_specs=pl.BlockSpec(memory_space=pltpu.VMEM),
        scratch_shapes=[pltpu.VMEM((2, 128, time_embed.shape[0]), BF16)],
        compiler_params=pltpu.CompilerParams(vmem_limit_bytes=32 * MIB),
        cost_estimate=pl.CostEstimate(flops=10**9, transcendentals=10**5, bytes_accessed=2 * MIB),
        name="prologue",
    )(
        own_scal, queries[0], key_proj[0], value_proj[0], cosine, sine,
        norm_gain, norm_bias, time_embed.reshape(-1, 128),
        gate_table.T, mod_table.T,
    )
    first, second, message = lax.optimization_barrier((first, second, message))
    with jax.named_scope("weights"):
        near_a = jnp.concatenate([first] + [send(first, dx=d) for d in range(1, 4)], 0)
        near_b = jnp.concatenate([second] + [send(second, dy=d) for d in range(1, 4)], 0)
        pieces = [near_a] + [send(near_a, dy=d) for d in range(1, 4)]
        pieces += [near_b] + [send(near_b, dx=d) for d in range(1, 4)]
    planes = [list(range(64)), list(range(64, 128))]
    received = lax.all_to_all(
        message, "seq", split_axis=0, concat_axis=0, tiled=True, axis_index_groups=planes
    )
    kv_own, q = pl.pallas_call(
        unpack_kernel,
        out_shape=(jax.ShapeDtypeStruct((64, 24, 128), BF16), jax.ShapeDtypeStruct((1536, 128), BF16)),
        in_specs=vmem(1),
        out_specs=tuple(vmem(2)),
        compiler_params=pltpu.CompilerParams(vmem_limit_bytes=16 * MIB),
        cost_estimate=pl.CostEstimate(flops=10**6, transcendentals=0, bytes_accessed=2 * MIB),
        name="unpack",
    )(received)
    kv_own = kv_own.reshape(1536, 128)
    flip_y = [(i, i ^ 64) for i in range(seq_count)]
    flip_core = [(i, i ^ 1) for i in range(seq_count)]
    kv_y = lax.ppermute(kv_own, "seq", flip_y)
    kv_core = lax.ppermute(kv_own, "seq", flip_core)
    kv_far = lax.ppermute(kv_y, "seq", flip_core)

    terms = received[:, 32:38, HALF : HALF + 48]
    terms_y = lax.ppermute(terms, "seq", flip_y)

    def scal_of(plane, part):
        return jnp.stack([plane, part, text_len[0]]).astype(jnp.int32)

    acc = attend(scal_of(y, core), q, kv_own, None, False)
    acc = attend(scal_of(y, 1 - core), q, kv_core, acc, False)
    acc = attend(scal_of(1 - y, core), q, kv_y, acc, False)
    answer = attend(scal_of(1 - y, 1 - core), q, kv_far, acc, True)
    returned = lax.all_to_all(
        answer, "seq", split_axis=0, concat_axis=0, tiled=True, axis_index_groups=planes
    )

    model_width = hidden.shape[2]
    terms = jnp.where(y == 0, jnp.stack([terms, terms_y]), jnp.stack([terms_y, terms]))
    terms = terms.astype(F32).reshape(seq_count, 2, 3, 48)
    vectors = terms[:, :, 0] + terms[:, :, 1] + terms[:, :, 2]
    modulation = vectors[:, 0].reshape(2, model_width)
    gate_vec = vectors[:, 1, :24].reshape(1, model_width)

    own_width = latent.shape[1] // 2
    own_latent = lax.dynamic_slice_in_dim(latent.T, cfg_place * own_width, own_width, 0)
    step_coefs = lax.dynamic_index_in_dim(solver_coef, step_index[0], axis=1, keepdims=False)
    kept = jnp.where(is_video.T, step_coefs[0] * own_latent, 0.0)
    moved = jnp.where(is_video.T, step_coefs[1], 0.0)
    bias = proj_bias[:, None]
    returned, gate_vec, modulation, kept, moved, bias = lax.optimization_barrier(
        (returned, gate_vec, modulation, kept, moved, bias)
    )
    place_scal = jnp.stack([core, ring_y, x]).astype(jnp.int32)
    own_part, other_part = pl.pallas_call(
        project_kernel,
        out_shape=(jax.ShapeDtypeStruct((rows, model_width), F32),) * 2,
        in_specs=smem(1) + vmem(9),
        out_specs=tuple(vmem(2)),
        scratch_shapes=[
            pltpu.VMEM((128, depth), BF16),
            pltpu.VMEM((model_width, 128), F32),
            pltpu.VMEM((128, model_width), F32),
        ],
        compiler_params=pltpu.CompilerParams(vmem_limit_bytes=32 * MIB),
        cost_estimate=pl.CostEstimate(flops=10**9, transcendentals=0, bytes_accessed=8 * MIB),
        name="project",
    )(place_scal, returned, *pieces)
    got_part = lax.ppermute(other_part, "seq", flip_core)
    own_pred, sent_pred = pl.pallas_call(
        final_kernel,
        out_shape=(jax.ShapeDtypeStruct((own_width, rows), F32),) * 2,
        in_specs=smem(1) + vmem(8),
        out_specs=tuple(vmem(2)),
        scratch_shapes=[pltpu.VMEM((2 * own_width, rows), F32)],
        compiler_params=pltpu.CompilerParams(vmem_limit_bytes=24 * MIB),
        cost_estimate=pl.CostEstimate(flops=10**8, transcendentals=0, bytes_accessed=2 * MIB),
        name="finish",
    )(
        cfg_place.reshape(1).astype(jnp.int32), own_part, got_part, hidden[0], gate_vec,
        modulation[0:1], modulation[1:2], proj_weight.T, bias,
    )
    partner = lax.ppermute(sent_pred, "cfg", [(0, 1), (1, 0)])
    is_cond = cfg_place == 0
    cond_pred = jnp.where(is_cond, own_pred, partner)
    uncond_pred = jnp.where(is_cond, partner, own_pred)
    guided = uncond_pred + GUIDANCE * (cond_pred - uncond_pred)
    return (kept + moved * guided).T


def solution(mesh):
    placed = (
        P("cfg", "seq", None), P("cfg", "seq", None), P("cfg", "seq", None), P("cfg", "seq", None),
        P(), P(), P(None, "seq"), P("cfg"), P(), P(None, "seq"), P(None, "seq"), P(None, ("cfg", "seq")),
        P(), P(), P("seq", None), P(), P(),
    )
    return jax.shard_map(
        on_device, mesh=mesh, in_specs=placed, out_specs=P("seq", "cfg"), check_vma=False
    )
```

```python
import functools

import jax
import jax.numpy as jnp
import numpy as np
from jax import lax
from jax.experimental import pallas as pl
from jax.experimental.pallas import tpu as pltpu
from jax.sharding import PartitionSpec as P

TEXT_SLOTS = 256
GUIDANCE = 6.0
HALF = 64
MIB = 1 << 20
F32 = jnp.float32
BF16 = jnp.bfloat16
NT = (((1,), (1,)), ((), ()))


def lane_iota(shape):
    return lax.broadcasted_iota(jnp.int32, shape, len(shape) - 1)


def vmem(n):
    return [pl.BlockSpec(memory_space=pltpu.VMEM)] * n


def smem(n):
    return [pl.BlockSpec(memory_space=pltpu.SMEM)] * n


def normed(stacked, gain, bias, ones):
    mean = jnp.dot(stacked.astype(BF16), ones.astype(BF16), preferred_element_type=F32) * (1.0 / 64)
    centred = stacked - mean
    var = jnp.dot(
        centred * centred, ones, preferred_element_type=F32, precision=lax.Precision.HIGHEST
    ) * (1.0 / 64)
    return centred * lax.rsqrt(var + 1e-6) * gain + bias


def rotated(values, cosine, sine):
    lane = lane_iota(values.shape)
    other = jnp.where(lane % 2 == 0, pltpu.roll(values, 127, 1), pltpu.roll(values, 1, 1))
    return (values * cosine + other * sine).astype(BF16).astype(F32)


def vector_kernel(emb_ref, gate_ref, mod_ref, out, table):
    emb = emb_ref[...].astype(F32)
    act = emb / (1.0 + jnp.exp(-emb))
    table[...] = jnp.zeros_like(table)
    table[0, HALF : HALF + mod_ref.shape[0]] = mod_ref[...]
    table[1, HALF : HALF + gate_ref.shape[0]] = gate_ref[...]
    row8 = lax.broadcasted_iota(jnp.int32, (8, 128), 0)
    sums = []
    for t in range(2):
        total = jnp.zeros((8, 128), F32)
        for k in range(act.shape[0]):
            part = jnp.broadcast_to(act[k : k + 1], (8, 128)).astype(BF16)
            total += lax.dot_general(part, table[t, :, 128 * k : 128 * k + 128], NT, preferred_element_type=F32)
        sums.append(total)
    out[...] = jnp.where(row8 == 0, sums[0], sums[1])


def prologue_kernel(
    scal, q_ref, k_ref, v_ref, cos_ref, sin_ref, gain_ref, bias_ref, own_vec, far_vec,
    send_ref,
):
    rows = q_ref.shape[0]
    blocks = q_ref.shape[1] // 128
    gain = jnp.concatenate([gain_ref[...]] * 2, axis=1)
    bias = jnp.concatenate([bias_ref[...]] * 2, axis=1)
    r = lax.broadcasted_iota(jnp.int32, (128, 128), 0)
    c = lax.broadcasted_iota(jnp.int32, (128, 128), 1)
    ones = jnp.where((r < HALF) == (c < HALF), 1.0, 0.0).astype(F32)
    cosine = jnp.concatenate([cos_ref[...]] * blocks, axis=0)
    sine = jnp.concatenate([sin_ref[...]] * blocks, axis=0)

    def stack(ref):
        x = ref[...].astype(F32)
        return jnp.concatenate([x[:, 128 * p : 128 * p + 128] for p in range(blocks)], axis=0)

    q_all = rotated(normed(stack(q_ref), gain[0:1], bias[0:1], ones), cosine, sine) * 0.125
    k_all = rotated(normed(stack(k_ref), gain[1:2], bias[1:2], ones), cosine, sine)
    token = scal[0] + lax.broadcasted_iota(jnp.int32, (rows, 128), 0)
    valid = (token >= TEXT_SLOTS) | (token < scal[1])
    lane = lane_iota((rows, 128))

    row8 = lax.broadcasted_iota(jnp.int32, (8, 128), 0)
    extra = jnp.zeros((8, 128), F32)
    for i, (ref, row) in enumerate(((own_vec, 0), (far_vec, 0), (own_vec, 1), (far_vec, 1))):
        value = jnp.broadcast_to(ref[row : row + 1], (8, 128))
        first = value.astype(BF16).astype(F32)
        second = (value - first).astype(BF16).astype(F32)
        extra = jnp.where(row8 == 2 * i, first, jnp.where(row8 == 2 * i + 1, second, extra))

    lane16 = lane_iota((16, 128))
    for p in range(blocks):
        qb = q_all[rows * p : rows * (p + 1)]
        kb = jnp.where(valid, k_all[rows * p : rows * (p + 1)], 0.0)
        vb = jnp.where(valid, v_ref[:, 128 * p : 128 * p + 128].astype(F32), 0.0)
        qr, kr, vr = (pltpu.roll(t, HALF, 1) for t in (qb, kb, vb))
        for odd in range(2):
            kv = jnp.where(lane < HALF, kr, vb) if odd else jnp.where(lane < HALF, kb, vr)
            low, high = (qr, qb) if odd else (qb, qr)
            for part in range(2):
                dest = 2 * (2 * p + odd) + part
                at = 24 * part
                send_ref[dest, 0:24] = kv[at : at + 24].astype(BF16)
                upper = jnp.concatenate([high[at + 16 : at + 24], extra], axis=0)
                send_ref[dest, 24:40] = jnp.where(lane16 < HALF, low[at : at + 16], upper).astype(BF16)


def unpack_kernel(recv_ref, kv_ref, q_ref):
    n = recv_ref.shape[0]
    kv_ref[...] = recv_ref[:, 0:24, :]
    low = recv_ref[:, 24:40, :].astype(F32).reshape(n * 16, 128)
    q_ref[0 : n * 16] = jnp.where(lane_iota(low.shape) < HALF, low, 0.0).astype(BF16)
    high = pltpu.roll(recv_ref[:, 24:32, :].astype(F32).reshape(n * 8, 128), HALF, 1)
    q_ref[n * 16 : n * 24] = jnp.where(lane_iota(high.shape) < HALF, high, 0.0).astype(BF16)


def attend_kernel(first, last, scal, q_ref, kv_ref, *rest):
    acc_in = None if first else rest[0]
    rest = rest if first else rest[1:]
    out_ref, va = rest[0], rest[1]
    acc = rest[2] if last else out_ref
    keys = kv_ref.shape[0]
    queries = q_ref.shape[0]
    lane = lane_iota((256, 128))
    n = lax.broadcasted_iota(jnp.int32, (256, 128), 0).astype(F32)
    source = jnp.floor((n + 0.5) * (1.0 / 24))
    token = (scal[0] * 64).astype(F32) * 48 + source * 48 + (scal[1] * 24).astype(F32) + (n - source * 24)
    valid = (token >= TEXT_SLOTS) | (token < scal[2].astype(F32))
    va[0:256] = jnp.where(lane < HALF, jnp.where(valid, 1.0, 0.0), kv_ref[0:256].astype(F32)).astype(BF16)
    big = lane_iota((keys - 256, 128))
    va[256:] = jnp.where(big < HALF, 1.0, kv_ref[256:].astype(F32)).astype(BF16)
    q_step, k_step = 768, 512

    def block(i, carry):
        at = pl.ds(pl.multiple_of(i * q_step, q_step), q_step)
        q = q_ref[at, :]
        total = None if first else acc_in[at, :]
        for k0 in range(0, keys, k_step):
            s = lax.dot_general(q, kv_ref[k0 : k0 + k_step], NT, preferred_element_type=F32)
            p = jnp.exp(s).astype(BF16)
            part = jnp.dot(p, va[k0 : k0 + k_step], preferred_element_type=F32)
            total = part if total is None else total + part
        acc[at, :] = total
        return carry

    lax.fori_loop(0, queries // q_step, block, 0)
    if last:
        n_src = out_ref.shape[0]

        def ratio(x):
            return x / pltpu.roll(x, HALF, 1)

        for base, size, to in ((0, 16, 0), (n_src * 16, 8, 16)):
            x = ratio(acc[base : base + n_src * size, :])
            back = pltpu.roll(x, HALF, 1).reshape(n_src // 2, 2, size, 128)
            x = x.reshape(n_src // 2, 2, size, 128)
            both = jnp.where(lane_iota((n_src // 2, size, 128)) < HALF, back[:, 0], x[:, 1])
            both = both.astype(BF16)
            for chip in range(n_src // 2):
                out_ref[2 * chip, to : to + size] = both[chip]
                out_ref[2 * chip + 1, to : to + size] = both[chip]


def attend(scal, q, kv, acc, last):
    first = acc is None
    keys, queries = kv.shape[0], q.shape[0]
    n_src = keys // 24
    out = jax.ShapeDtypeStruct((n_src, 24, 128), BF16) if last else jax.ShapeDtypeStruct((queries, 128), F32)
    scratch = [pltpu.VMEM((keys, 128), BF16)]
    if last:
        scratch.append(pltpu.VMEM((queries, 128), F32))
    args = (scal, q, kv) if first else (scal, q, kv, acc)
    return pl.pallas_call(
        functools.partial(attend_kernel, first, last),
        out_shape=out,
        in_specs=smem(1) + vmem(len(args) - 1),
        out_specs=pl.BlockSpec(memory_space=pltpu.VMEM),
        scratch_shapes=scratch,
        cost_estimate=pl.CostEstimate(
            flops=4 * keys * queries * 256, transcendentals=keys * queries, bytes_accessed=2 * MIB
        ),
        compiler_params=pltpu.CompilerParams(vmem_limit_bytes=24 * MIB),
        name="attend",
    )(*args)


def project_kernel(scal, recv_ref, *rest):
    pieces, (hidden_ref, gate_ref) = rest[:8], rest[8:10]
    own_ref, other_ref, att, total, natural, held, sem = rest[10:]
    copy = pltpu.make_async_copy(hidden_ref, held, sem)
    copy.start()
    core, ring_y, ring_x = scal[0], scal[1], scal[2]
    heads = recv_ref.shape[0] // 4
    base = core * (2 * heads)
    lane = lane_iota((24, 128))
    att[96:128] = jnp.zeros((32, att.shape[1]), BF16)
    for m in range(heads // 2):
        for part in range(2):
            a = recv_ref[base + 4 * m + part].astype(F32)
            b = recv_ref[base + 4 * m + 2 + part].astype(F32)
            cols = slice(128 * m, 128 * m + 128)
            att[24 * part : 24 * part + 24, cols] = jnp.where(lane < HALF, a, pltpu.roll(b, HALF, 1)).astype(BF16)
            att[48 + 24 * part : 72 + 24 * part, cols] = jnp.where(lane < HALF, pltpu.roll(a, HALF, 1), b).astype(BF16)
    quarter = att.shape[1] // 2
    for colour in range(2):
        rhs = att[:, colour * quarter : (colour + 1) * quarter]
        for far in range(4):
            ref = pieces[4 * colour + far]
            for near in range(4):
                dy, dx = (far, near) if colour == 0 else (near, far)
                y = lax.rem(ring_y - dy + 4, 4)
                x = lax.rem(ring_x - dx + 4, 4)
                res = lax.dot_general(ref[192 * near : 192 * near + 192], rhs, NT, preferred_element_type=F32)
                at = pl.ds(pl.multiple_of((y * 4 + x) * 192, 192), 192)
                total[at, :] = res if colour == 0 else total[at, :] + res
    for b in range(total.shape[0] // 128):
        natural[:, 128 * b : 128 * b + 128] = total[128 * b : 128 * b + 128, :].T
    own = natural[pl.ds(pl.multiple_of(core * 48, 8), 48), :]
    copy.wait()
    own_ref[...] = held[...].astype(F32) + gate_ref[...] * own
    other_ref[...] = natural[pl.ds(pl.multiple_of((1 - core) * 48, 8), 48), :]


def final_kernel(cfg, own, other, gate, shift, scale, weight, bias, out, sent, both, held, sem):
    copy = pltpu.make_async_copy(weight, held, sem)
    copy.start()
    x = own[...] + gate[...] * other[...]
    centred = x - jnp.mean(x, axis=1, keepdims=True)
    var = jnp.mean(centred * centred, axis=1, keepdims=True)
    y = centred * lax.rsqrt(var + 1e-5) * (1.0 + scale[...]) + shift[...]
    copy.wait()
    both[...] = lax.dot_general(held[...], y.astype(BF16), NT, preferred_element_type=F32) + bias[...]
    width = out.shape[0]
    out[...] = both[pl.ds(pl.multiple_of(cfg[0] * width, 8), width), :]
    sent[...] = both[pl.ds(pl.multiple_of((1 - cfg[0]) * width, 8), width), :]


def on_device(
    hidden, queries, key_proj, value_proj, norm_gain, norm_bias, positions, text_len, time_embed,
    gate_table, mod_table, out_weight, proj_weight, proj_bias, latent, solver_coef, step_index,
):
    both = ("cfg", "seq")
    seq_count = lax.axis_size("seq")
    cfg_place, place = lax.axis_index("cfg"), lax.axis_index("seq")
    core, z, x, y = place % 2, place // 2 % 8, place // 16 % 4, place // 64
    ring_y = cfg_place * 2 + y
    rows = queries.shape[1]

    def send(value, dx=0, dy=0, dz=0, dc=0):
        pairs = []
        for i in range(2 * seq_count):
            c_, z_, x_, y_ = i % 2, i // 2 % 8, i // 16 % 4, i // 64
            target = (y_ + dy) % 4 * 64 + (x_ + dx) % 4 * 16 + (z_ + dz) % 8 * 2 + (c_ + dc) % 2
            pairs.append((i, target))
        return lax.ppermute(value, both, pairs)

    with jax.named_scope("weights"):
        columns = out_weight.T
        width, depth = columns.shape[0], columns.shape[1] // 2
        halves = columns.reshape(width, 2, depth).transpose(1, 0, 2)
        shares = jnp.broadcast_to(halves[None], (8, 2, width, depth)).reshape(16, width, depth)
        rings = [list(range(i, i + 16)) for i in range(0, seq_count, 16)]
        along_z = lax.all_to_all(
            shares, "seq", split_axis=0, concat_axis=0, tiled=True, axis_index_groups=rings
        ).reshape(16 * width, depth)
        first, second = along_z[:, : depth // 2], along_z[:, depth // 2 :]

    pair = np.arange(128) % 64 // 2
    index = np.where(pair < 8, pair, np.where(pair < 20, pair - 8, pair - 20))
    width = np.where(pair < 8, 16.0, 24.0)
    freq = jnp.asarray(10000.0 ** (-2.0 * index / width), F32)[None, :]
    pos = positions.astype(F32)[:, :, None]
    angle = jnp.where((pair < 8)[None], pos[0], jnp.where((pair < 20)[None], pos[1], pos[2])) * freq
    is_video = (place * rows + jnp.arange(rows) >= TEXT_SLOTS)[:, None]
    cosine = jnp.where(is_video, jnp.cos(angle), 1.0)
    sign = jnp.asarray(np.where(np.arange(128) % 2 == 0, -1.0, 1.0), F32)[None, :]
    sine = jnp.where(is_video, jnp.sin(angle) * sign, 0.0)
    own_scal = jnp.stack([place * rows, text_len[0]]).astype(jnp.int32)
    flip_y = [(i, i ^ 64) for i in range(seq_count)]
    flip_core = [(i, i ^ 1) for i in range(seq_count)]
    own_vec = pl.pallas_call(
        vector_kernel,
        out_shape=jax.ShapeDtypeStruct((8, 128), F32),
        in_specs=vmem(3),
        out_specs=pl.BlockSpec(memory_space=pltpu.VMEM),
        scratch_shapes=[pltpu.VMEM((2, 128, time_embed.shape[0]), BF16)],
        compiler_params=pltpu.CompilerParams(vmem_limit_bytes=8 * MIB),
        cost_estimate=pl.CostEstimate(flops=10**6, transcendentals=0, bytes_accessed=2**17),
        name="vectors",
    )(time_embed.reshape(-1, 128), gate_table.T, mod_table.T)
    far_vec = lax.ppermute(own_vec, "seq", flip_y)
    message = pl.pallas_call(
        prologue_kernel,
        out_shape=jax.ShapeDtypeStruct((64, 40, 128), BF16),
        in_specs=smem(1) + vmem(9),
        out_specs=pl.BlockSpec(memory_space=pltpu.VMEM),
        compiler_params=pltpu.CompilerParams(vmem_limit_bytes=32 * MIB),
        cost_estimate=pl.CostEstimate(flops=10**9, transcendentals=10**5, bytes_accessed=2 * MIB),
        name="prologue",
    )(
        own_scal, queries[0], key_proj[0], value_proj[0], cosine, sine,
        norm_gain, norm_bias, own_vec, far_vec,
    )
    first, second, message = lax.optimization_barrier((first, second, message))
    with jax.named_scope("weights"):
        near_a = jnp.concatenate([first] + [send(first, dx=d) for d in range(1, 4)], 0)
        near_b = jnp.concatenate([second] + [send(second, dy=d) for d in range(1, 4)], 0)
        pieces = [near_a] + [send(near_a, dy=d) for d in range(1, 4)]
        pieces += [near_b] + [send(near_b, dx=d) for d in range(1, 4)]
    planes = [list(range(64)), list(range(64, 128))]
    received = lax.all_to_all(
        message, "seq", split_axis=0, concat_axis=0, tiled=True, axis_index_groups=planes
    )
    kv_own, q = pl.pallas_call(
        unpack_kernel,
        out_shape=(jax.ShapeDtypeStruct((64, 24, 128), BF16), jax.ShapeDtypeStruct((1536, 128), BF16)),
        in_specs=vmem(1),
        out_specs=tuple(vmem(2)),
        compiler_params=pltpu.CompilerParams(vmem_limit_bytes=16 * MIB),
        cost_estimate=pl.CostEstimate(flops=10**6, transcendentals=0, bytes_accessed=2 * MIB),
        name="unpack",
    )(received)
    kv_own = kv_own.reshape(1536, 128)
    kv_y = lax.ppermute(kv_own, "seq", flip_y)
    kv_core = lax.ppermute(kv_own, "seq", flip_core)
    kv_far = lax.ppermute(kv_y, "seq", flip_core)

    def scal_of(plane, part):
        return jnp.stack([plane, part, text_len[0]]).astype(jnp.int32)

    acc = attend(scal_of(y, core), q, kv_own, None, False)
    acc = attend(scal_of(y, 1 - core), q, kv_core, acc, False)
    acc = attend(scal_of(1 - y, core), q, kv_y, acc, False)
    answer = attend(scal_of(1 - y, 1 - core), q, kv_far, acc, True)
    returned = lax.all_to_all(
        answer, "seq", split_axis=0, concat_axis=0, tiled=True, axis_index_groups=planes
    )

    model_width = hidden.shape[2]
    terms = received[:, 32:40, HALF : HALF + 48].astype(F32).reshape(64, 2, 2, 2, 48)
    terms = (terms[:, :, :, 0] + terms[:, :, :, 1]).transpose(1, 2, 0, 3)
    vectors = jnp.where(y == 0, terms, terms[:, ::-1])
    modulation = vectors[0].reshape(2, model_width)
    gate_vec = vectors[1, :, :, :24].reshape(1, model_width)

    own_width = latent.shape[1] // 2
    own_latent = lax.dynamic_slice_in_dim(latent.T, cfg_place * own_width, own_width, 0)
    step_coefs = lax.dynamic_index_in_dim(solver_coef, step_index[0], axis=1, keepdims=False)
    kept = jnp.where(is_video.T, step_coefs[0] * own_latent, 0.0)
    moved = jnp.where(is_video.T, step_coefs[1], 0.0)
    bias = proj_bias[:, None]
    returned, gate_vec, modulation, kept, moved, bias = lax.optimization_barrier(
        (returned, gate_vec, modulation, kept, moved, bias)
    )
    place_scal = jnp.stack([core, ring_y, x]).astype(jnp.int32)
    part_shape = jax.ShapeDtypeStruct((rows, model_width), F32)
    own_part, other_part = pl.pallas_call(
        project_kernel,
        out_shape=(part_shape, part_shape),
        in_specs=smem(1)
        + vmem(9)
        + [pl.BlockSpec(memory_space=pltpu.HBM), vmem(1)[0]],
        out_specs=tuple(vmem(2)),
        scratch_shapes=[
            pltpu.VMEM((128, depth), BF16),
            pltpu.VMEM((model_width, 128), F32),
            pltpu.VMEM((128, model_width), F32),
            pltpu.VMEM((rows, model_width), BF16),
            pltpu.SemaphoreType.DMA(()),
        ],
        compiler_params=pltpu.CompilerParams(vmem_limit_bytes=32 * MIB),
        cost_estimate=pl.CostEstimate(flops=10**9, transcendentals=0, bytes_accessed=8 * MIB),
        name="project",
    )(place_scal, returned, *pieces, hidden[0], gate_vec)
    got_part = lax.ppermute(other_part, "seq", flip_core)
    own_pred, sent_pred = pl.pallas_call(
        final_kernel,
        out_shape=(jax.ShapeDtypeStruct((own_width, rows), F32),) * 2,
        in_specs=smem(1) + vmem(5) + [pl.BlockSpec(memory_space=pltpu.HBM), vmem(1)[0]],
        out_specs=tuple(vmem(2)),
        scratch_shapes=[
            pltpu.VMEM((2 * own_width, rows), F32),
            pltpu.VMEM((2 * own_width, model_width), BF16),
            pltpu.SemaphoreType.DMA(()),
        ],
        compiler_params=pltpu.CompilerParams(vmem_limit_bytes=24 * MIB),
        cost_estimate=pl.CostEstimate(flops=10**8, transcendentals=0, bytes_accessed=2 * MIB),
        name="finish",
    )(
        cfg_place.reshape(1).astype(jnp.int32), own_part, got_part, gate_vec,
        modulation[0:1], modulation[1:2], proj_weight.T, bias,
    )
    partner = lax.ppermute(sent_pred, "cfg", [(0, 1), (1, 0)])
    is_cond = cfg_place == 0
    cond_pred = jnp.where(is_cond, own_pred, partner)
    uncond_pred = jnp.where(is_cond, partner, own_pred)
    guided = uncond_pred + GUIDANCE * (cond_pred - uncond_pred)
    return (kept + moved * guided).T


def solution(mesh):
    placed = (
        P("cfg", "seq", None), P("cfg", "seq", None), P("cfg", "seq", None), P("cfg", "seq", None),
        P(), P(), P(None, "seq"), P("cfg"), P(), P(None, "seq"), P(None, "seq"), P(None, ("cfg", "seq")),
        P(), P(), P("seq", None), P(), P(),
    )
    return jax.shard_map(
        on_device, mesh=mesh, in_specs=placed, out_specs=P("seq", "cfg"), check_vma=False
    )
```
